512 devices in a mesh: section: 32 (over y, x, core), ctx: 16 (over z).
Axes of the slice: x: 4, y: 4, z: 16, core: 2. Of those that a mesh axis runs over, the one named last changes fastest.
Arguments:
- streams: bfloat16 [32, 2048, 5120], P('section', 'ctx'), may hold values from -6 to 6
- conv_weight: bfloat16 [32, 4, 5120], P('section'), may hold values from -3 to 3
- beta_logit: float32 [32, 2048, 16], P('section', 'ctx'), may hold values from -12 to 3
- gate_log: float32 [32, 2048, 8], P('section', 'ctx'), may hold values from -2 to 0
- norm_gain: float32 [32, 1024], P('section'), may hold values from 0.25 to 1.75
- w_out: bfloat16 [32, 1024, 2048], P('section', None, 'ctx'), may hold values from -0.1875 to 0.1875
Outputs:
- handed: bfloat16 [32, 2048, 2048], P('section', 'ctx')
The draws below stay inside these ranges and needn't reach their ends.
All inputs are finite; a program needn't handle non-finite values.
Results may differ from the reference program's by a relative error of at most 0.0049.
Values may be sent and summed in bfloat16 or wider, within the bound.
A program may use at most 128 MiB of HBM per device.

```python
import math
import jax
import jax.numpy as jnp
from jax import lax

D = 2048
HEAD_TOTAL = 8
HK = 128
STEPS = 2
CONV = 4
SPAN = 128
TOK_DEV = 128
TOKEN_TOTAL = 2048
RELAY_SECTIONS = 32
HD = 1024
CH = 5120


def log_uniform(random_subkey, out_shape, low_end, high_end):
    return jnp.exp(jax.random.uniform(random_subkey, out_shape, jnp.float32, math.log(low_end), math.log(high_end)))


def fast_heads(key):
    fast_share = 0.5
    picked = jax.random.uniform(jax.random.fold_in(key, 11), (RELAY_SECTIONS, 1, HEAD_TOTAL), jnp.float32)
    return picked < fast_share


def shard_factor(random_subkey, lanes):
    factor = log_uniform(random_subkey, (RELAY_SECTIONS, TOKEN_TOTAL // TOK_DEV, lanes), 0.5, 2.0)
    return jnp.repeat(factor, TOK_DEV, axis=1)


def draw_gate_log(key, part):
    is_fast = fast_heads(key)
    random_subkey = jax.random.fold_in(key, 23)
    fast_rate = log_uniform(jax.random.fold_in(random_subkey, 1), (RELAY_SECTIONS, 1, HEAD_TOTAL), 0.8, 1.3) / min(40, TOK_DEV)
    slow_rate = log_uniform(jax.random.fold_in(random_subkey, 2), (RELAY_SECTIONS, 1, HEAD_TOTAL), 0.05, 0.3) / TOKEN_TOTAL
    decay_rates = jnp.where(is_fast, fast_rate, slow_rate)
    roughness = log_uniform(jax.random.fold_in(random_subkey, 3), (RELAY_SECTIONS, TOKEN_TOTAL, HEAD_TOTAL), 0.5, 2.0)
    spike_positions = jax.random.randint(jax.random.fold_in(random_subkey, 4), (RELAY_SECTIONS, 2, 1), 0, TOKEN_TOTAL)
    spike_matches = jnp.sum((jnp.arange(TOKEN_TOTAL)[None, None, :] == spike_positions).astype(jnp.float32), axis=1)
    spike_removals = jax.random.uniform(jax.random.fold_in(random_subkey, 5), (RELAY_SECTIONS, TOKEN_TOTAL, HEAD_TOTAL), jnp.float32, math.log(0.55), math.log(0.8))
    gentle_portion = decay_rates * shard_factor(jax.random.fold_in(random_subkey, 6), HEAD_TOTAL) * roughness
    return spike_matches[..., None] * spike_removals - gentle_portion


def draw_beta_logit(key, part):
    is_fast = jnp.tile(fast_heads(key), (1, 1, STEPS))
    random_subkey = jax.random.fold_in(key, 37)
    fast_size = log_uniform(jax.random.fold_in(random_subkey, 1), (RELAY_SECTIONS, 1, STEPS * HEAD_TOTAL), 0.2, 0.7)
    slow_size = log_uniform(jax.random.fold_in(random_subkey, 2), (RELAY_SECTIONS, 1, STEPS * HEAD_TOTAL), 0.05, 0.25) * HK / TOKEN_TOTAL
    roughness = log_uniform(jax.random.fold_in(random_subkey, 4), (RELAY_SECTIONS, TOKEN_TOTAL, STEPS * HEAD_TOTAL), 0.5, 2.0)
    sizes_now = jnp.where(is_fast, fast_size, slow_size) * shard_factor(jax.random.fold_in(random_subkey, 3), STEPS * HEAD_TOTAL) * roughness
    sizes_now = jnp.minimum(sizes_now, 0.95)
    return jnp.log(sizes_now) - jnp.log1p(-sizes_now)


def steps_of(rng, dims, shards, low, top_value):
    def one(axis_at, shards_of):
        draws = jax.random.uniform(jax.random.fold_in(jax.random.fold_in(rng, 6), axis_at), (shards_of,), jnp.float32, low / len(shards), top_value / len(shards))
        return jnp.repeat(jnp.exp(draws), dims[axis_at] // shards_of).reshape((-1,) + (1,) * (len(dims) - axis_at - 1))

    gain = one(*shards[0])
    for cut in shards[1:]:
        gain = gain * one(*cut)
    return gain


def gaussian(own_key, shape, scale, limit, cuts=(), kind=jnp.bfloat16):
    entries = scale * jax.random.normal(own_key, shape, jnp.float32)
    if cuts:
        entries = entries * steps_of(own_key, shape, cuts, -0.22, 0.18)
    return jnp.clip(entries, -limit, limit).astype(kind)


def setup_inputs(seed: int = 0) -> dict:
    seeds = jax.random.split(jax.random.key(seed), 7)
    streams = gaussian(seeds[0], (RELAY_SECTIONS, TOKEN_TOTAL, CH), 1.0, 6.0, ((0, 32), (1, 16)))
    conv_weight = gaussian(seeds[1], (RELAY_SECTIONS, CONV, CH), CONV ** -0.5, 3.0, ((0, 32),))
    beta_logit = draw_beta_logit(jax.random.fold_in(seeds[6], 71), 0)
    gate_log = draw_gate_log(jax.random.fold_in(seeds[6], 71), 0)
    norm_gain = jnp.clip(1.0 + 0.15 * jax.random.normal(seeds[4], (RELAY_SECTIONS, HD), jnp.float32), 0.25, 1.75)
    w_out = gaussian(seeds[5], (RELAY_SECTIONS, HD, D), HD ** -0.5, 0.1875, ((0, 32), (2, 16)))
    return {"streams": streams, "conv_weight": conv_weight, "beta_logit": beta_logit, "gate_log": gate_log, "norm_gain": norm_gain, "w_out": w_out}


highest = lax.Precision.HIGHEST

def mix_taps(extended, tap_weights):
    tok_count = extended.shape[0] - tap_weights.shape[0] + 1
    summed = jnp.zeros((tok_count, extended.shape[1]), jnp.float32)
    for offset in range(tap_weights.shape[0]):
        summed = summed + tap_weights[offset].astype(jnp.float32) * extended[offset:offset + tok_count].astype(jnp.float32)
    return jax.nn.silu(summed)

def unit_rows(vectors):
    return vectors * lax.rsqrt(lax.optimization_barrier(jnp.sum(vectors * vectors, axis=-1, keepdims=True)) + 1e-06)

def head_major(active, beta_logit, gate_log):
    tok_count = active.shape[0]
    head_width = HEAD_TOTAL * HK
    queries = unit_rows(active[:, :head_width].reshape(tok_count, HEAD_TOTAL, HK)).transpose(1, 0, 2)
    keys_all = unit_rows(active[:, head_width:(1 + STEPS) * head_width].reshape(tok_count, STEPS, HEAD_TOTAL, HK))
    keys_all = keys_all.transpose(2, 0, 1, 3).reshape(HEAD_TOTAL, tok_count * STEPS, HK)
    values_all = active[:, (1 + STEPS) * head_width:].reshape(tok_count, STEPS, HEAD_TOTAL, HK)
    values_all = values_all.transpose(2, 0, 1, 3).reshape(HEAD_TOTAL, tok_count * STEPS, HK)
    step_size = jax.nn.sigmoid(beta_logit.reshape(tok_count, STEPS, HEAD_TOTAL)).transpose(2, 0, 1).reshape(HEAD_TOTAL, tok_count * STEPS)
    opening = (lax.broadcasted_iota(jnp.int32, (1, STEPS, 1), 1) == 0).astype(gate_log.dtype)
    log_gate = (gate_log[:, None, :] * opening).transpose(2, 0, 1).reshape(HEAD_TOTAL, tok_count * STEPS)
    return (queries, keys_all, values_all, step_size, log_gate)

def span_terms(queries, keys_all, values_all, step_size, log_gate):
    head_count, virtual, head_dim = keys_all.shape
    blocks = virtual // SPAN
    per_block = SPAN // STEPS
    queries = queries.reshape(head_count, blocks, per_block, head_dim)
    keys_all = keys_all.reshape(head_count, blocks, SPAN, head_dim)
    values_all = values_all.reshape(head_count, blocks, SPAN, head_dim)
    step_size = step_size.reshape(head_count, blocks, SPAN)
    cumulate = jnp.cumsum(log_gate.reshape(head_count, blocks, SPAN), axis=-1)
    query_log = cumulate[..., STEPS - 1::STEPS]
    row_index = lax.broadcasted_iota(jnp.int32, (SPAN, SPAN), 0)
    col_index = lax.broadcasted_iota(jnp.int32, (SPAN, SPAN), 1)
    strict = col_index < row_index
    spread = cumulate[..., :, None] - cumulate[..., None, :]
    damping = jnp.where(strict, jnp.exp(jnp.where(strict, spread, 0.0)), 0.0)
    key_inner = jnp.einsum('hcid,hcjd->hcij', keys_all, keys_all, precision=highest)
    unit_lower = jnp.eye(SPAN, dtype=key_inner.dtype) + step_size[..., :, None] * damping * key_inner
    right_sides = jnp.concatenate([step_size[..., None] * values_all, (step_size * jnp.exp(cumulate))[..., None] * keys_all], axis=-1)
    solved = jax.scipy.linalg.solve_triangular(unit_lower, right_sides, lower=True, unit_diagonal=True)
    value_part = solved[..., :head_dim]
    key_part = solved[..., head_dim:]
    to_end = keys_all * jnp.exp(cumulate[..., -1:] - cumulate)[..., None]
    carried = jnp.exp(cumulate[..., -1])[..., None, None] * jnp.eye(head_dim, dtype=key_inner.dtype)
    carried = carried - jnp.einsum('hcid,hcie->hcde', to_end, key_part, precision=highest)
    written = jnp.einsum('hcid,hcie->hcde', to_end, value_part, precision=highest)
    query_row = lax.broadcasted_iota(jnp.int32, (per_block, SPAN), 0) * STEPS + STEPS - 1
    query_col = lax.broadcasted_iota(jnp.int32, (per_block, SPAN), 1)
    allowed = query_col <= query_row
    query_spread = query_log[..., :, None] - cumulate[..., None, :]
    query_damping = jnp.where(allowed, jnp.exp(jnp.where(allowed, query_spread, 0.0)), 0.0)
    scores = jnp.einsum('hcpd,hcid->hcpi', queries, keys_all, precision=highest) * query_damping
    direct = jnp.einsum('hcpi,hcie->hcpe', scores, value_part, precision=highest)
    reach_map = queries * jnp.exp(query_log)[..., None] - jnp.einsum('hcpi,hcie->hcpe', scores, key_part, precision=highest)
    return (jnp.moveaxis(carried, 1, 0), jnp.moveaxis(written, 1, 0), jnp.moveaxis(direct, 1, 0), jnp.moveaxis(reach_map, 1, 0))

def advance(state_now, piece_terms):
    carried, written, direct, reach_map = piece_terms
    span_out = direct + jnp.einsum('hpd,hde->hpe', reach_map, state_now, precision=highest)
    state_now = jnp.einsum('hde,hef->hdf', carried, state_now, precision=highest) + written
    return (state_now, span_out)

def normalize(outputs, norm_gain):
    tok_count = outputs.shape[0]
    inverse_rms = lax.rsqrt(lax.optimization_barrier(jnp.mean(outputs * outputs, axis=-1, keepdims=True)) + 1e-05)
    return (outputs * inverse_rms * norm_gain.reshape(HEAD_TOTAL, HK)).reshape(tok_count, HEAD_TOTAL * HK).astype(jnp.bfloat16)

def mixer_layer(streams, conv_weight, beta_logit, gate_log, norm_gain, w_out):
    zero_rows = jnp.zeros((CONV - 1, streams.shape[1]), streams.dtype)
    active = mix_taps(jnp.concatenate([zero_rows, streams], axis=0), conv_weight)
    span_parts = span_terms(*head_major(active, beta_logit, gate_log))
    state_start = jnp.zeros((HEAD_TOTAL, HK, HK), jnp.float32)
    _, outputs = lax.scan(advance, state_start, span_parts)
    outputs = outputs.transpose(0, 2, 1, 3).reshape(streams.shape[0], HEAD_TOTAL, HK)
    normed = normalize(outputs, norm_gain)
    return jnp.dot(normed.astype(jnp.float32), w_out.astype(jnp.float32), preferred_element_type=jnp.float32).astype(jnp.bfloat16)

def reference(streams, conv_weight, beta_logit, gate_log, norm_gain, w_out):
    mixed_rows = lax.map(lambda section_args: mixer_layer(*section_args), (streams, conv_weight, beta_logit, gate_log, norm_gain, w_out))
    return jnp.roll(mixed_rows, 1, axis=0)
```

```python
import functools

import jax
import jax.numpy as jnp
from jax import lax
from jax.experimental import pallas as pl
from jax.experimental.pallas import tpu as pltpu
from jax.sharding import PartitionSpec as P

HEAD_TOTAL = 8
HK = 128
STEPS = 2
CONV = 4
TOK = 128
PAIR = 2
MESH = pl.DeviceIdType.MESH
highest = lax.Precision.HIGHEST

NN = (((1,), (0,)), ((), ()))
NT = (((1,), (1,)), ((), ()))
TN = (((0,), (0,)), ((), ()))


def split(a):
    high = a.astype(jnp.bfloat16)
    return high, (a - high.astype(jnp.float32)).astype(jnp.bfloat16)


def dot(a, b, dims=NN):
    return lax.dot_general(a, b, dims, preferred_element_type=jnp.float32)


def dot3(a, b, dims=NN):
    (ah, al), (bh, bl) = a, b
    return dot(ah, bh, dims) + (dot(ah, bl, dims) + dot(al, bh, dims))


def unit_rows(vectors):
    return vectors * lax.rsqrt(jnp.sum(vectors * vectors, axis=-1, keepdims=True) + 1e-06)


def local_terms(heads):
    both = STEPS * TOK
    row = lax.broadcasted_iota(jnp.int32, (both, both), 0)
    col = lax.broadcasted_iota(jnp.int32, (both, both), 1)
    row_tok, col_tok = row & (TOK - 1), col & (TOK - 1)
    tok_row = lax.broadcasted_iota(jnp.int32, (TOK, TOK), 0)
    tok_col = lax.broadcasted_iota(jnp.int32, (TOK, TOK), 1)
    before = (col_tok < row_tok) | ((col_tok == row_tok) & (col < row))
    keys, sizes, inner, damp = [], [], [], []
    for q, k0, k1, v0, v1, b0, b1, c_col, c_row in heads:
        key = jnp.concatenate([k0, k1], axis=0)
        keys.append(key)
        sizes.append(jnp.concatenate([b0, b1], axis=0))
        kept = jnp.where(tok_col <= tok_row, jnp.exp(jnp.minimum(c_col - c_row, 0.0)), 0.0)
        damp.append(jnp.concatenate([kept, kept], axis=1))
    key_parts = [split(key) for key in keys]
    lower = []
    for parts, size, kept in zip(key_parts, sizes, damp):
        grid = dot3(parts, parts, NT)
        wide = jnp.concatenate([kept, kept], axis=0)
        lower.append(jnp.where(before, size * wide * grid, 0.0))
    eye = (row == col).astype(jnp.float32)
    same = row_tok == col_tok
    inverse = [eye - jnp.where(same, m, 0.0) for m in lower]
    shift = 0
    while (1 << shift) < TOK:
        joined = ((row_tok >> (shift + 1)) == (col_tok >> (shift + 1))) & (
            (row_tok >> shift) != (col_tok >> shift)
        )
        inv_parts = [split(x) for x in inverse]
        crosses = [split(jnp.where(joined, m, 0.0)) for m in lower]
        halves = [split(dot3(c, x)) for c, x in zip(crosses, inv_parts)]
        inverse = [x - dot3(p, y) for x, p, y in zip(inverse, inv_parts, halves)]
        shift += 1
    results = []
    for (q, k0, k1, v0, v1, b0, b1, c_col, c_row), key, parts, kept, x in zip(
        heads, keys, key_parts, damp, inverse
    ):
        grown = jnp.exp(c_col)
        right = jnp.concatenate(
            [
                jnp.concatenate([b0 * v0, b1 * v1], axis=0),
                jnp.concatenate([(b0 * grown) * k0, (b1 * grown) * k1], axis=0),
            ],
            axis=1,
        )
        solved = split(dot3(split(x), split(right)))
        last = c_col[TOK - 1 :, :]
        rest = jnp.exp(last - c_col)
        ends = split(jnp.concatenate([k0 * rest, k1 * rest], axis=0))
        moved = dot3(ends, solved, TN)
        scores = split(dot3(split(q), parts, NT) * kept)
        seen = dot3(scores, solved)
        written, taken = moved[:, :HK], moved[:, HK:]
        direct, reach = seen[:, :HK], q * grown - seen[:, HK:]
        results.append((taken, written, direct, reach, jnp.exp(last)))
    return results


def local_kernel(
    q_ref, k0_ref, k1_ref, v0_ref, v1_ref,
    qr, k0r, k1r, v0r, v1r,
    qw, k0w, k1w, v0w, v1w,
    beta_ref, gate_ref,
    taken_ref, written_ref, direct_ref, reach_ref, keep_ref,
    ext,
):
    first = pl.program_id(0) * PAIR

    def act(x_ref, rim_ref, w_ref):
        ext[8 - (CONV - 1) : 8, :] = rim_ref[...].astype(jnp.float32)
        ext[8:, :] = x_ref[...].astype(jnp.float32)
        summed = jnp.zeros((TOK, PAIR * HK), jnp.float32)
        taps = w_ref[...].astype(jnp.float32)
        for i in range(CONV):
            start = 8 - (CONV - 1) + i
            summed = summed + taps[i : i + 1] * ext[start : start + TOK, :]
        return summed * jax.nn.sigmoid(summed)

    queries = act(q_ref, qr, qw)
    key_0, key_1 = act(k0_ref, k0r, k0w), act(k1_ref, k1r, k1w)
    value_0, value_1 = act(v0_ref, v0r, v0w), act(v1_ref, v1r, v1w)
    tok_row = lax.broadcasted_iota(jnp.int32, (TOK, TOK), 0)
    tok_col = lax.broadcasted_iota(jnp.int32, (TOK, TOK), 1)
    ones = (tok_col <= tok_row).astype(jnp.float32)
    gates = gate_ref[...]
    c_cols = lax.dot_general(ones, gates, NN, precision=highest, preferred_element_type=jnp.float32)
    c_rows = lax.dot_general(
        gates, ones, (((0,), (1,)), ((), ())), precision=highest, preferred_element_type=jnp.float32
    )
    betas = jax.nn.sigmoid(beta_ref[...])

    def column(values, which):
        lane = lax.broadcasted_iota(jnp.int32, values.shape, 1)
        return jnp.sum(jnp.where(lane == which, values, 0.0), axis=1, keepdims=True)

    def picked_row(values, which):
        lane = lax.broadcasted_iota(jnp.int32, values.shape, 0)
        return jnp.sum(jnp.where(lane == which, values, 0.0), axis=0, keepdims=True)

    heads = []
    for p in range(PAIR):
        at = slice(p * HK, (p + 1) * HK)
        heads.append(
            (
                unit_rows(queries[:, at]),
                unit_rows(key_0[:, at]),
                unit_rows(key_1[:, at]),
                value_0[:, at],
                value_1[:, at],
                column(betas, first + p),
                column(betas, HEAD_TOTAL + first + p),
                column(c_cols, first + p),
                picked_row(c_rows, first + p),
            )
        )
    for p, (taken, written, direct, reach, keep) in enumerate(local_terms(heads)):
        taken_ref[p] = taken
        written_ref[p] = written
        direct_ref[p] = direct
        reach_ref[p] = reach
        keep_ref[p] = jnp.broadcast_to(keep, (8, HK))


def local_call(rows, rim, taps, beta, gate):
    groups = HEAD_TOTAL // PAIR
    width = PAIR * HK

    def specs(height):
        return [
            pl.BlockSpec((height, width), functools.partial(lambda n, g: (0, n * groups + g), n))
            for n in range(1 + 2 * STEPS)
        ]

    square = jax.ShapeDtypeStruct((HEAD_TOTAL, HK, HK), jnp.float32)
    square_spec = pl.BlockSpec((PAIR, HK, HK), lambda g: (g, 0, 0))
    return pl.pallas_call(
        local_kernel,
        grid=(groups,),
        in_specs=specs(TOK)
        + specs(CONV - 1)
        + specs(CONV)
        + [
            pl.BlockSpec((TOK, STEPS * HEAD_TOTAL), lambda g: (0, 0)),
            pl.BlockSpec((TOK, HEAD_TOTAL), lambda g: (0, 0)),
        ],
        out_specs=[square_spec] * 4 + [pl.BlockSpec((PAIR, 8, HK), lambda g: (g, 0, 0))],
        out_shape=[square] * 4 + [jax.ShapeDtypeStruct((HEAD_TOTAL, 8, HK), jnp.float32)],
        scratch_shapes=[pltpu.VMEM((TOK + 8, width), jnp.float32)],
        name="local_terms",
        cost_estimate=pl.CostEstimate(
            flops=8 * 50 * 2 * 256**3, bytes_accessed=4_000_000, transcendentals=1_000_000
        ),
    )(*([rows] * 5 + [rim] * 5 + [taps] * 5), beta, gate)


def chain_kernel(
    count, taken_ref, written_ref, direct_ref, reach_ref, keep_ref, gain_ref, normed_ref,
    entering, leaving, send_sem, recv_sem,
):
    mine = lax.axis_index("ctx")
    after, prior = lax.rem(mine + 1, count), lax.rem(mine + count - 1, count)
    barrier = pltpu.get_barrier_semaphore()
    for other in (after, prior):
        pl.semaphore_signal(barrier, inc=1, device_id={"ctx": other}, device_id_type=MESH)
    pl.semaphore_wait(barrier, 2)

    def hop(h):
        return pltpu.make_async_remote_copy(
            src_ref=leaving.at[h],
            dst_ref=entering.at[h],
            send_sem=send_sem.at[h],
            recv_sem=recv_sem.at[h],
            device_id={"ctx": after},
            device_id_type=MESH,
        )

    @pl.when(mine == 0)
    def _():
        entering[...] = jnp.zeros_like(entering)

    for h in range(HEAD_TOTAL):
        @pl.when(mine > 0)
        def _():
            hop(h).wait_recv()

        state = entering[h]
        parts = split(state)
        step = keep_ref[h][:1] * state - dot3(split(taken_ref[h]), parts) + written_ref[h]

        @pl.when(mine < count - 1)
        def _():
            leaving[h] = step
            hop(h).start()

        out = direct_ref[h] + dot3(split(reach_ref[h]), parts)
        scale = lax.rsqrt(jnp.mean(out * out, axis=-1, keepdims=True) + 1e-05)
        at = slice(h * HK, (h + 1) * HK)
        normed_ref[:, at] = (out * scale * gain_ref[:, at]).astype(jnp.bfloat16)

    @pl.when(mine < count - 1)
    def _():
        for h in range(HEAD_TOTAL):
            hop(h).wait_send()


def chain_call(count, terms, gain):
    whole = pl.BlockSpec(memory_space=pltpu.VMEM)
    return pl.pallas_call(
        functools.partial(chain_kernel, count),
        in_specs=[whole] * 6,
        out_specs=whole,
        out_shape=jax.ShapeDtypeStruct((TOK, HEAD_TOTAL * HK), jnp.bfloat16),
        scratch_shapes=[
            pltpu.VMEM((HEAD_TOTAL, HK, HK), jnp.float32),
            pltpu.VMEM((HEAD_TOTAL, HK, HK), jnp.float32),
            pltpu.SemaphoreType.DMA((HEAD_TOTAL,)),
            pltpu.SemaphoreType.DMA((HEAD_TOTAL,)),
        ],
        compiler_params=pltpu.CompilerParams(collective_id=0, has_side_effects=True),
        name="state_chain",
        cost_estimate=pl.CostEstimate(
            flops=50_000_000_000, bytes_accessed=3_000_000, transcendentals=0
        ),
    )(*terms, gain)


def on_device(streams, conv_weight, beta_logit, gate_log, norm_gain, w_out):
    count = lax.axis_size("ctx")
    sections = lax.axis_size("section")
    rows = streams[0]
    rim = lax.ppermute(
        rows[rows.shape[0] - (CONV - 1) :], "ctx", [(s, s + 1) for s in range(count - 1)]
    )
    columns = lax.all_gather(w_out[0], "ctx", axis=1, tiled=True)
    terms = local_call(rows, rim, conv_weight[0], beta_logit[0], gate_log[0])
    normed = chain_call(count, terms, norm_gain)
    mixed = jnp.dot(normed, columns, preferred_element_type=jnp.float32).astype(jnp.bfloat16)
    return lax.ppermute(
        mixed[None], "section", [(s, (s + 1) % sections) for s in range(sections)]
    )


def solution(mesh):
    placed = (
        P("section", "ctx", None),
        P("section", None, None),
        P("section", "ctx", None),
        P("section", "ctx", None),
        P("section", None),
        P("section", None, "ctx"),
    )
    return jax.shard_map(
        on_device, mesh=mesh, in_specs=placed, out_specs=P("section", "ctx", None), check_vma=False
    )
```

```python
import functools

import jax
import jax.numpy as jnp
from jax import lax
from jax.experimental import pallas as pl
from jax.experimental.pallas import tpu as pltpu
from jax.sharding import PartitionSpec as P

HEAD_TOTAL = 8
HK = 128
STEPS = 2
CONV = 4
TOK = 128
PAIR = 2
MESH = pl.DeviceIdType.MESH
highest = lax.Precision.HIGHEST

NN = (((1,), (0,)), ((), ()))
NT = (((1,), (1,)), ((), ()))
TN = (((0,), (0,)), ((), ()))


def split(a):
    high = a.astype(jnp.bfloat16)
    return high, (a - high.astype(jnp.float32)).astype(jnp.bfloat16)


def dot(a, b, dims=NN):
    return lax.dot_general(a, b, dims, preferred_element_type=jnp.float32)


def dot3(a, b, dims=NN):
    (ah, al), (bh, bl) = a, b
    return dot(ah, bh, dims) + (dot(ah, bl, dims) + dot(al, bh, dims))


def unit_rows(vectors):
    return vectors * lax.rsqrt(jnp.sum(vectors * vectors, axis=-1, keepdims=True) + 1e-06)


def local_terms(heads):
    both = STEPS * TOK
    row = lax.broadcasted_iota(jnp.int32, (both, both), 0)
    col = lax.broadcasted_iota(jnp.int32, (both, both), 1)
    row_tok, col_tok = row & (TOK - 1), col & (TOK - 1)
    tok_row = lax.broadcasted_iota(jnp.int32, (TOK, TOK), 0)
    tok_col = lax.broadcasted_iota(jnp.int32, (TOK, TOK), 1)
    before = (col_tok < row_tok) | ((col_tok == row_tok) & (col < row))
    keys, sizes, inner, damp = [], [], [], []
    for q, k0, k1, v0, v1, b0, b1, c_col, c_row in heads:
        key = jnp.concatenate([k0, k1], axis=0)
        keys.append(key)
        sizes.append(jnp.concatenate([b0, b1], axis=0))
        kept = jnp.where(tok_col <= tok_row, jnp.exp(jnp.minimum(c_col - c_row, 0.0)), 0.0)
        damp.append(jnp.concatenate([kept, kept], axis=1))
    key_parts = [split(key) for key in keys]
    lower = []
    for parts, size, kept in zip(key_parts, sizes, damp):
        grid = dot3(parts, parts, NT)
        wide = jnp.concatenate([kept, kept], axis=0)
        lower.append(jnp.where(before, size * wide * grid, 0.0))
    eye = (row == col).astype(jnp.float32)
    same = row_tok == col_tok
    inverse = [eye - jnp.where(same, m, 0.0) for m in lower]
    shift = 0
    while (1 << shift) < TOK:
        joined = ((row_tok >> (shift + 1)) == (col_tok >> (shift + 1))) & (
            (row_tok >> shift) != (col_tok >> shift)
        )
        rounded = [x.astype(jnp.bfloat16) for x in inverse]
        crosses = [jnp.where(joined, m, 0.0).astype(jnp.bfloat16) for m in lower]
        halves = [dot(c, x).astype(jnp.bfloat16) for c, x in zip(crosses, rounded)]
        inverse = [x - dot(p, y) for x, p, y in zip(inverse, rounded, halves)]
        shift += 1
    results = []
    for (q, k0, k1, v0, v1, b0, b1, c_col, c_row), m, parts, kept, x in zip(
        heads, lower, key_parts, damp, inverse
    ):
        grown = jnp.exp(c_col)
        right = jnp.concatenate(
            [
                jnp.concatenate([b0 * v0, b1 * v1], axis=0),
                jnp.concatenate([(b0 * grown) * k0, (b1 * grown) * k1], axis=0),
            ],
            axis=1,
        )
        near = x.astype(jnp.bfloat16)
        solved = dot(near, right.astype(jnp.bfloat16))
        miss = (right - solved) - dot3(split(m), split(solved))
        solved = split(solved + dot(near, miss.astype(jnp.bfloat16)))
        last = c_col[TOK - 1 :, :]
        rest = jnp.exp(last - c_col)
        ends = split(jnp.concatenate([k0 * rest, k1 * rest], axis=0))
        moved = dot3(ends, solved, TN)
        scores = split(dot3(split(q), parts, NT) * kept)
        seen = dot3(scores, solved)
        written, taken = moved[:, :HK], moved[:, HK:]
        direct, reach = seen[:, :HK], q * grown - seen[:, HK:]
        results.append((taken, written, direct, reach, jnp.exp(last)))
    return results


def whole_kernel(
    count, sections,
    rows_ref, taps_ref, beta_ref, gate_ref, gain_ref, w_ref, out_ref,
    ext, rim, taken_hi, taken_lo, reach_hi, reach_lo, written, direct, keep,
    entering, leaving, ready, arrived, gathered,
    rim_sems, w_sems, send_sem, recv_sem, ready_send, ready_recv,
    back_send, back_recv, fore_send, fore_recv,
):
    mine, section = lax.axis_index("ctx"), lax.axis_index("section")
    after, prior = lax.rem(mine + 1, count), lax.rem(mine + count - 1, count)
    onward, behind = lax.rem(section + 1, sections), lax.rem(section + sections - 1, sections)
    fore_steps = (count - 1) // 3
    back_steps = count - 1 - fore_steps
    half_rows = w_ref.shape[0] // 2

    def remote(source, target, sends, receives, **where):
        return pltpu.make_async_remote_copy(
            src_ref=source, dst_ref=target, send_sem=sends, recv_sem=receives,
            device_id=where, device_id_type=MESH,
        )

    barrier = pltpu.get_barrier_semaphore()
    for where in ({"ctx": after}, {"ctx": prior}, {"section": onward}, {"section": behind}):
        pl.semaphore_signal(barrier, inc=1, device_id=where, device_id_type=MESH)
    pl.semaphore_wait(barrier, 4)

    edge = remote(rows_ref.at[TOK - 16 :], rim, rim_sems.at[0], rim_sems.at[1], ctx=after)
    own = remote(w_ref, gathered.at[mine], w_sems.at[0], w_sems.at[1], section=onward)

    @pl.when(mine < count - 1)
    def _():
        edge.start()

    own.start()

    def ring(send, receive, step, half, owner, target):
        block = gathered.at[owner, pl.ds(pl.multiple_of(half * half_rows, half_rows), half_rows)]
        return remote(block, block, send.at[step, half], receive.at[step, half], ctx=target)

    def back(step, half):
        return ring(back_send, back_recv, step, half, lax.rem(mine + step, count), prior)

    def fore(step, half):
        return ring(fore_send, fore_recv, step, half, lax.rem(mine + count - step, count), after)

    def relay(at, carry):
        step, half = lax.div(at, 2), lax.rem(at, 2)
        back(step - 1, half).wait_recv()
        back(step, half).start()

        @pl.when(step < fore_steps)
        def _():
            fore(step - 1, half).wait_recv()
            fore(step, half).start()

        return carry

    tok_row = lax.broadcasted_iota(jnp.int32, (TOK, TOK), 0)
    tok_col = lax.broadcasted_iota(jnp.int32, (TOK, TOK), 1)
    ones = (tok_col <= tok_row).astype(jnp.float32)
    eye = (tok_col == tok_row).astype(jnp.float32)
    gates = gate_ref[...]

    def exact(a, b):
        return lax.dot_general(a, b, NT, precision=highest, preferred_element_type=jnp.float32)

    c_cols, c_rows = exact(ones, gates), exact(gates, ones)
    betas = exact(eye, jax.nn.sigmoid(beta_ref[...]))

    def column(values, which):
        lane = lax.broadcasted_iota(jnp.int32, values.shape, 1)
        return jnp.sum(jnp.where(lane == which, values, 0.0), axis=1, keepdims=True)

    def picked_row(values, which):
        lane = lax.broadcasted_iota(jnp.int32, values.shape, 0)
        return jnp.sum(jnp.where(lane == which, values, 0.0), axis=0, keepdims=True)

    @pl.when(mine == 0)
    def _():
        rim[...] = jnp.zeros_like(rim)
        entering[...] = jnp.zeros_like(entering)

    @pl.when(mine > 0)
    def _():
        edge.wait_recv()

    width = PAIR * HK

    def group(g, carry):
        first = g * PAIR

        def act(n):
            at = pl.ds(pl.multiple_of(n * (HEAD_TOTAL * HK) + g * width, width), width)
            ext[:8, :] = rim[8:, at].astype(jnp.float32)
            ext[8:, :] = rows_ref[:, at].astype(jnp.float32)
            summed = jnp.zeros((TOK, width), jnp.float32)
            taps = taps_ref[:, at].astype(jnp.float32)
            for i in range(CONV):
                start = 8 - (CONV - 1) + i
                summed = summed + taps[i : i + 1] * ext[start : start + TOK, :]
            return summed * jax.nn.sigmoid(summed)

        queries, key_0, key_1, value_0, value_1 = [act(n) for n in range(1 + 2 * STEPS)]
        heads = []
        for p in range(PAIR):
            at = slice(p * HK, (p + 1) * HK)
            heads.append(
                (
                    unit_rows(queries[:, at]),
                    unit_rows(key_0[:, at]),
                    unit_rows(key_1[:, at]),
                    value_0[:, at],
                    value_1[:, at],
                    column(betas, first + p),
                    column(betas, HEAD_TOTAL + first + p),
                    column(c_cols, first + p),
                    picked_row(c_rows, first + p),
                )
            )
        for p, (took, wrote, seen, reach, kept) in enumerate(local_terms(heads)):
            h = first + p
            taken_hi[h], taken_lo[h] = split(took)
            reach_hi[h], reach_lo[h] = split(reach)
            written[h] = wrote
            direct[h] = seen
            keep[h] = jnp.broadcast_to(kept, (8, HK))

        @pl.when(g == 0)
        def _():
            own.wait_recv()
            for half in range(2):
                back(0, half).start()
                fore(0, half).start()

        return carry

    lax.fori_loop(0, HEAD_TOTAL // PAIR, group, 0)

    lead = jnp.minimum(4 + 2 * lax.div(mine, 2), 2 * back_steps)
    lax.fori_loop(2, lead, relay, 0)

    def hop(h):
        return remote(leaving.at[h], entering.at[h], send_sem.at[h], recv_sem.at[h], ctx=after)

    def share(h):
        return remote(ready.at[h], arrived.at[h], ready_send.at[h], ready_recv.at[h], section=onward)

    for h in range(HEAD_TOTAL):
        @pl.when(mine > 0)
        def _():
            hop(h).wait_recv()

        state = entering[h]
        parts = split(state)

        @pl.when(mine < count - 1)
        def _():
            step = dot3((taken_hi[h], taken_lo[h]), parts)
            leaving[h] = (keep[h][:1] * state + written[h]) - step
            hop(h).start()

        made = direct[h] + dot3((reach_hi[h], reach_lo[h]), parts)
        scale = lax.rsqrt(jnp.mean(made * made, axis=-1, keepdims=True) + 1e-05)
        gain = gain_ref[:, h * HK : (h + 1) * HK]
        ready[h] = (made * scale * gain).astype(jnp.bfloat16)
        share(h).start()

    lax.fori_loop(lead, 2 * back_steps, relay, 0)
    for half in range(2):
        back(back_steps - 1, half).wait_recv()
        fore(fore_steps - 1, half).wait_recv()
    for h in range(HEAD_TOTAL):
        share(h).wait_recv()
    normed = jnp.concatenate([arrived[h] for h in range(HEAD_TOTAL)], axis=1)

    def columns(n, carry):
        block = jnp.concatenate([gathered[2 * n], gathered[2 * n + 1]], axis=1)
        wide = block.shape[1]
        out_ref[:, pl.ds(pl.multiple_of(n * wide, wide), wide)] = dot(normed, block).astype(
            jnp.bfloat16
        )
        return carry

    lax.fori_loop(0, count // 2, columns, 0)

    own.wait_send()

    @pl.when(mine < count - 1)
    def _():
        edge.wait_send()
        for h in range(HEAD_TOTAL):
            hop(h).wait_send()

    for h in range(HEAD_TOTAL):
        share(h).wait_send()
    for half in range(2):
        for step in range(back_steps):
            back(step, half).wait_send()
        for step in range(fore_steps):
            fore(step, half).wait_send()


def on_device(streams, conv_weight, beta_logit, gate_log, norm_gain, w_out):
    count, sections = lax.axis_size("ctx"), lax.axis_size("section")
    fore_steps = (count - 1) // 3
    back_steps = count - 1 - fore_steps
    heads = (HEAD_TOTAL, HK, HK)
    depth, share = w_out.shape[1:]
    whole = pl.BlockSpec(memory_space=pltpu.VMEM)
    dma = pltpu.SemaphoreType.DMA
    mixed = pl.pallas_call(
        functools.partial(whole_kernel, count, sections),
        in_specs=[whole] * 6,
        out_specs=whole,
        out_shape=jax.ShapeDtypeStruct((TOK, count * share), jnp.bfloat16),
        scratch_shapes=[
            pltpu.VMEM((TOK + 8, PAIR * HK), jnp.float32),
            pltpu.VMEM((16, streams.shape[2]), jnp.bfloat16),
            pltpu.VMEM(heads, jnp.bfloat16),
            pltpu.VMEM(heads, jnp.bfloat16),
            pltpu.VMEM(heads, jnp.bfloat16),
            pltpu.VMEM(heads, jnp.bfloat16),
            pltpu.VMEM(heads, jnp.float32),
            pltpu.VMEM(heads, jnp.float32),
            pltpu.VMEM((HEAD_TOTAL, 8, HK), jnp.float32),
            pltpu.VMEM(heads, jnp.float32),
            pltpu.VMEM(heads, jnp.float32),
            pltpu.VMEM(heads, jnp.bfloat16),
            pltpu.VMEM(heads, jnp.bfloat16),
            pltpu.VMEM((count, depth, share), jnp.bfloat16),
            dma((2,)),
            dma((2,)),
            dma((HEAD_TOTAL,)),
            dma((HEAD_TOTAL,)),
            dma((HEAD_TOTAL,)),
            dma((HEAD_TOTAL,)),
            dma((back_steps, 2)),
            dma((back_steps, 2)),
            dma((fore_steps, 2)),
            dma((fore_steps, 2)),
        ],
        compiler_params=pltpu.CompilerParams(
            collective_id=0, has_side_effects=True, vmem_limit_bytes=60 * 2**20
        ),
        name="whole_mixer",
    )(streams[0], conv_weight[0], beta_logit[0].T, gate_log[0].T, norm_gain, w_out[0])
    return mixed[None]


def solution(mesh):
    placed = (
        P("section", "ctx", None),
        P("section", None, None),
        P("section", "ctx", None),
        P("section", "ctx", None),
        P("section", None),
        P("section", None, "ctx"),
    )
    return jax.shard_map(
        on_device, mesh=mesh, in_specs=placed, out_specs=P("section", "ctx", None), check_vma=False
    )
```

```python
import functools

import jax
import jax.numpy as jnp
from jax import lax
from jax.experimental import pallas as pl
from jax.experimental.pallas import tpu as pltpu
from jax.sharding import PartitionSpec as P

HEAD_TOTAL = 8
HK = 128
STEPS = 2
CONV = 4
TOK = 128
PAIR = 2
MESH = pl.DeviceIdType.MESH
highest = lax.Precision.HIGHEST

NN = (((1,), (0,)), ((), ()))
NT = (((1,), (1,)), ((), ()))
TN = (((0,), (0,)), ((), ()))


def split(a):
    high = a.astype(jnp.bfloat16)
    return high, (a - high.astype(jnp.float32)).astype(jnp.bfloat16)


def dot(a, b, dims=NN):
    return lax.dot_general(a, b, dims, preferred_element_type=jnp.float32)


def dot3(a, b, dims=NN):
    (ah, al), (bh, bl) = a, b
    return dot(ah, bh, dims) + (dot(ah, bl, dims) + dot(al, bh, dims))


def unit_rows(vectors):
    return vectors * lax.rsqrt(jnp.sum(vectors * vectors, axis=-1, keepdims=True) + 1e-06)


def local_terms(heads):
    half = TOK // 2
    row = lax.broadcasted_iota(jnp.int32, (TOK, TOK), 0)
    col = lax.broadcasted_iota(jnp.int32, (TOK, TOK), 1)
    row_tok, col_tok = row & (half - 1), col & (half - 1)
    same = row_tok == col_tok
    before = (col_tok < row_tok) | (same & (col < row))
    eye = (row == col).astype(jnp.float32)

    def halves(first, second):
        return [
            jnp.concatenate([first[at : at + half], second[at : at + half]], axis=0)
            for at in (0, half)
        ]

    keys, sizes, cols, rows, grids = [], [], [], [], []
    for q, k0, k1, v0, v1, b0, b1, c_col, c_row in heads:
        keys.append([split(part) for part in halves(k0, k1)])
        sizes.append(halves(b0, b1))
        cols.append(halves(c_col, c_col))
        rows.append(
            [jnp.concatenate([c_row[:, at : at + half]] * 2, axis=1) for at in (0, half)]
        )
        (early, late) = keys[-1]
        grids.append((dot3(early, early, NT), dot3(late, late, NT), dot3(late, early, NT)))

    def faded(n, i, j, grid):
        return sizes[n][i] * jnp.exp(jnp.minimum(cols[n][i] - rows[n][j], 0.0)) * grid

    lower, below = [], []
    for n, (first, second, cross) in enumerate(grids):
        lower.append(jnp.where(before, faded(n, 0, 0, first), 0.0))
        lower.append(jnp.where(before, faded(n, 1, 1, second), 0.0))
        below.append(split(faded(n, 1, 0, cross)))
    inverse = [eye - jnp.where(same, m, 0.0) for m in lower]
    shift = 0
    while (1 << shift) < half:
        joined = ((row_tok >> (shift + 1)) == (col_tok >> (shift + 1))) & (
            (row_tok >> shift) != (col_tok >> shift)
        )
        rounded = [x.astype(jnp.bfloat16) for x in inverse]
        crosses = [jnp.where(joined, m, 0.0).astype(jnp.bfloat16) for m in lower]
        products = [dot(c, x).astype(jnp.bfloat16) for c, x in zip(crosses, rounded)]
        inverse = [x - dot(p, y) for x, p, y in zip(inverse, rounded, products)]
        shift += 1
    near = [x.astype(jnp.bfloat16) for x in inverse]
    lower = [split(m) for m in lower]

    def solve(ms, xs, sides):
        got = [dot(x, side.astype(jnp.bfloat16)) for x, side in zip(xs, sides)]
        miss = [(side - s) - dot3(m, split(s)) for side, s, m in zip(sides, got, ms)]
        return [split(s + dot(x, e.astype(jnp.bfloat16))) for s, x, e in zip(got, xs, miss)]

    sides = []
    for n, (q, k0, k1, v0, v1, b0, b1, c_col, c_row) in enumerate(heads):
        grown = jnp.exp(c_col)
        values, scaled = halves(b0 * v0, b1 * v1), halves((b0 * grown) * k0, (b1 * grown) * k1)
        sides.append([jnp.concatenate([v, k], axis=1) for v, k in zip(values, scaled)])
    tops = solve(lower[::2], near[::2], [side[0] for side in sides])
    bottoms = solve(
        lower[1::2],
        near[1::2],
        [side[1] - dot3(m, top) for side, m, top in zip(sides, below, tops)],
    )
    score_col = lax.broadcasted_iota(jnp.int32, (TOK, STEPS * TOK), 1)
    score_tok = (score_col // TOK) * half + (score_col & (half - 1))
    allowed = score_tok <= lax.broadcasted_iota(jnp.int32, (TOK, STEPS * TOK), 0)
    results = []
    for n, (q, k0, k1, v0, v1, b0, b1, c_col, c_row) in enumerate(heads):
        solved = [jnp.concatenate(pair, axis=0) for pair in zip(tops[n], bottoms[n])]
        last = c_col[TOK - 1 :, :]
        rest = jnp.exp(last - c_col)
        ends = split(jnp.concatenate(halves(k0 * rest, k1 * rest), axis=0))
        moved = dot3(ends, solved, TN)
        both = [jnp.concatenate(pair, axis=0) for pair in zip(*keys[n])]
        fade = jnp.exp(jnp.minimum(c_col - jnp.concatenate(rows[n], axis=1), 0.0))
        scores = split(jnp.where(allowed, dot3(split(q), both, NT) * fade, 0.0))
        seen = dot3(scores, solved)
        written, taken = moved[:, :HK], moved[:, HK:]
        direct, reach = seen[:, :HK], q * jnp.exp(c_col) - seen[:, HK:]
        results.append((taken, written, direct, reach, jnp.exp(last)))
    return results


def whole_kernel(
    count, sections,
    rows_ref, taps_ref, beta_ref, gate_ref, gain_ref, w_ref, out_ref,
    ext, rim, taken_hi, taken_lo, reach_hi, reach_lo, written, direct, keep,
    entering, leaving, ready, arrived, gathered,
    rim_sems, w_sems, send_sem, recv_sem, ready_send, ready_recv,
    back_send, back_recv, fore_send, fore_recv,
):
    mine, section = lax.axis_index("ctx"), lax.axis_index("section")
    after, prior = lax.rem(mine + 1, count), lax.rem(mine + count - 1, count)
    onward, behind = lax.rem(section + 1, sections), lax.rem(section + sections - 1, sections)
    fore_steps = (count - 1) // 3
    back_steps = count - 1 - fore_steps
    half_rows = w_ref.shape[0] // 2

    def remote(source, target, sends, receives, **where):
        return pltpu.make_async_remote_copy(
            src_ref=source, dst_ref=target, send_sem=sends, recv_sem=receives,
            device_id=where, device_id_type=MESH,
        )

    barrier = pltpu.get_barrier_semaphore()
    for where in ({"ctx": after}, {"ctx": prior}, {"section": onward}, {"section": behind}):
        pl.semaphore_signal(barrier, inc=1, device_id=where, device_id_type=MESH)
    pl.semaphore_wait(barrier, 4)

    edge = remote(rows_ref.at[TOK - 16 :], rim, rim_sems.at[0], rim_sems.at[1], ctx=after)
    own = remote(w_ref, gathered.at[mine], w_sems.at[0], w_sems.at[1], section=onward)

    @pl.when(mine < count - 1)
    def _():
        edge.start()

    own.start()

    def ring(send, receive, step, half, owner, target):
        block = gathered.at[owner, pl.ds(pl.multiple_of(half * half_rows, half_rows), half_rows)]
        return remote(block, block, send.at[step, half], receive.at[step, half], ctx=target)

    def back(step, half):
        return ring(back_send, back_recv, step, half, lax.rem(mine + step, count), prior)

    def fore(step, half):
        return ring(fore_send, fore_recv, step, half, lax.rem(mine + count - step, count), after)

    def relay(at, carry):
        step, half = lax.div(at, 2), lax.rem(at, 2)
        back(step - 1, half).wait_recv()
        back(step, half).start()

        @pl.when(step < fore_steps)
        def _():
            fore(step - 1, half).wait_recv()
            fore(step, half).start()

        return carry

    tok_row = lax.broadcasted_iota(jnp.int32, (TOK, TOK), 0)
    tok_col = lax.broadcasted_iota(jnp.int32, (TOK, TOK), 1)
    ones = (tok_col <= tok_row).astype(jnp.float32)
    eye = (tok_col == tok_row).astype(jnp.float32)
    gates = gate_ref[...]

    def exact(a, b):
        return lax.dot_general(a, b, NT, precision=highest, preferred_element_type=jnp.float32)

    c_cols, c_rows = exact(ones, gates), exact(gates, ones)
    betas = exact(eye, jax.nn.sigmoid(beta_ref[...]))

    def column(values, which):
        lane = lax.broadcasted_iota(jnp.int32, values.shape, 1)
        return jnp.sum(jnp.where(lane == which, values, 0.0), axis=1, keepdims=True)

    def picked_row(values, which):
        lane = lax.broadcasted_iota(jnp.int32, values.shape, 0)
        return jnp.sum(jnp.where(lane == which, values, 0.0), axis=0, keepdims=True)

    @pl.when(mine == 0)
    def _():
        rim[...] = jnp.zeros_like(rim)
        entering[...] = jnp.zeros_like(entering)

    @pl.when(mine > 0)
    def _():
        edge.wait_recv()

    width = PAIR * HK
    groups = HEAD_TOTAL // PAIR

    def hop(h):
        return remote(leaving.at[h], entering.at[h], send_sem.at[h], recv_sem.at[h], ctx=after)

    def share(h):
        return remote(ready.at[h], arrived.at[h], ready_send.at[h], ready_recv.at[h], section=onward)

    def chain(h):
        @pl.when(mine > 0)
        def _():
            hop(h).wait_recv()

        state = entering[h]
        parts = split(state)

        @pl.when(mine < count - 1)
        def _():
            step = dot3((taken_hi[h], taken_lo[h]), parts)
            leaving[h] = (keep[h][:1] * state + written[h]) - step
            hop(h).start()

        made = direct[h] + dot3((reach_hi[h], reach_lo[h]), parts)
        scale = lax.rsqrt(jnp.mean(made * made, axis=-1, keepdims=True) + 1e-05)
        gain = gain_ref[:, pl.ds(pl.multiple_of(h * HK, HK), HK)]
        ready[h] = (made * scale * gain).astype(jnp.bfloat16)
        share(h).start()

    def chain_group(g, carry):
        for p in range(PAIR):
            chain(g * PAIR + p)
        return carry

    def group(g, carry):
        first = g * PAIR

        def act(n):
            at = pl.ds(pl.multiple_of(n * (HEAD_TOTAL * HK) + g * width, width), width)
            ext[:8, :] = rim[8:, at].astype(jnp.float32)
            ext[8:, :] = rows_ref[:, at].astype(jnp.float32)
            summed = jnp.zeros((TOK, width), jnp.float32)
            taps = taps_ref[:, at].astype(jnp.float32)
            for i in range(CONV):
                start = 8 - (CONV - 1) + i
                summed = summed + taps[i : i + 1] * ext[start : start + TOK, :]
            return summed * jax.nn.sigmoid(summed)

        queries, key_0, key_1, value_0, value_1 = [act(n) for n in range(1 + 2 * STEPS)]
        heads = []
        for p in range(PAIR):
            at = slice(p * HK, (p + 1) * HK)
            heads.append(
                (
                    unit_rows(queries[:, at]),
                    unit_rows(key_0[:, at]),
                    unit_rows(key_1[:, at]),
                    value_0[:, at],
                    value_1[:, at],
                    column(betas, first + p),
                    column(betas, HEAD_TOTAL + first + p),
                    column(c_cols, first + p),
                    picked_row(c_rows, first + p),
                )
            )
        for p, (took, wrote, seen, reach, kept) in enumerate(local_terms(heads)):
            h = first + p
            taken_hi[h], taken_lo[h] = split(took)
            reach_hi[h], reach_lo[h] = split(reach)
            written[h] = wrote
            direct[h] = seen
            keep[h] = jnp.broadcast_to(kept, (8, HK))

        @pl.when(g == 0)
        def _():
            own.wait_recv()
            for half in range(2):
                back(0, half).start()
                fore(0, half).start()

        @pl.when(g > 0)
        def _():
            for half in range(2):
                relay(2 * g + half, 0)

        @pl.when(g >= mine)
        def _():
            chain_group(g - mine, 0)

        return carry

    lax.fori_loop(0, groups, group, 0)

    lead = jnp.minimum(2 * groups + 2 * lax.div(mine, 2), 2 * back_steps)
    lax.fori_loop(2 * groups, lead, relay, 0)

    lax.fori_loop(jnp.maximum(groups - mine, 0), groups, chain_group, 0)

    lax.fori_loop(lead, 2 * back_steps, relay, 0)
    for half in range(2):
        back(back_steps - 1, half).wait_recv()
        fore(fore_steps - 1, half).wait_recv()
    for h in range(HEAD_TOTAL):
        share(h).wait_recv()
    normed = jnp.concatenate([arrived[h] for h in range(HEAD_TOTAL)], axis=1)

    def columns(n, carry):
        block = jnp.concatenate([gathered[2 * n], gathered[2 * n + 1]], axis=1)
        wide = block.shape[1]
        out_ref[:, pl.ds(pl.multiple_of(n * wide, wide), wide)] = dot(normed, block).astype(
            jnp.bfloat16
        )
        return carry

    lax.fori_loop(0, count // 2, columns, 0)

    own.wait_send()

    @pl.when(mine < count - 1)
    def _():
        edge.wait_send()
        for h in range(HEAD_TOTAL):
            hop(h).wait_send()

    for h in range(HEAD_TOTAL):
        share(h).wait_send()
    for half in range(2):
        for step in range(back_steps):
            back(step, half).wait_send()
        for step in range(fore_steps):
            fore(step, half).wait_send()


def on_device(streams, conv_weight, beta_logit, gate_log, norm_gain, w_out):
    count, sections = lax.axis_size("ctx"), lax.axis_size("section")
    fore_steps = (count - 1) // 3
    back_steps = count - 1 - fore_steps
    heads = (HEAD_TOTAL, HK, HK)
    depth, share = w_out.shape[1:]
    whole = pl.BlockSpec(memory_space=pltpu.VMEM)
    dma = pltpu.SemaphoreType.DMA
    mixed = pl.pallas_call(
        functools.partial(whole_kernel, count, sections),
        in_specs=[whole] * 6,
        out_specs=whole,
        out_shape=jax.ShapeDtypeStruct((TOK, count * share), jnp.bfloat16),
        scratch_shapes=[
            pltpu.VMEM((TOK + 8, PAIR * HK), jnp.float32),
            pltpu.VMEM((16, streams.shape[2]), jnp.bfloat16),
            pltpu.VMEM(heads, jnp.bfloat16),
            pltpu.VMEM(heads, jnp.bfloat16),
            pltpu.VMEM(heads, jnp.bfloat16),
            pltpu.VMEM(heads, jnp.bfloat16),
            pltpu.VMEM(heads, jnp.float32),
            pltpu.VMEM(heads, jnp.float32),
            pltpu.VMEM((HEAD_TOTAL, 8, HK), jnp.float32),
            pltpu.VMEM(heads, jnp.float32),
            pltpu.VMEM(heads, jnp.float32),
            pltpu.VMEM(heads, jnp.bfloat16),
            pltpu.VMEM(heads, jnp.bfloat16),
            pltpu.VMEM((count, depth, share), jnp.bfloat16),
            dma((2,)),
            dma((2,)),
            dma((HEAD_TOTAL,)),
            dma((HEAD_TOTAL,)),
            dma((HEAD_TOTAL,)),
            dma((HEAD_TOTAL,)),
            dma((back_steps, 2)),
            dma((back_steps, 2)),
            dma((fore_steps, 2)),
            dma((fore_steps, 2)),
        ],
        compiler_params=pltpu.CompilerParams(
            collective_id=0, has_side_effects=True, vmem_limit_bytes=60 * 2**20
        ),
        name="whole_mixer",
    )(streams[0], conv_weight[0], beta_logit[0].T, gate_log[0].T, norm_gain, w_out[0])
    return mixed[None]


def solution(mesh):
    placed = (
        P("section", "ctx", None),
        P("section", None, None),
        P("section", "ctx", None),
        P("section", "ctx", None),
        P("section", None),
        P("section", None, "ctx"),
    )
    return jax.shard_map(
        on_device, mesh=mesh, in_specs=placed, out_specs=P("section", "ctx", None), check_vma=False
    )
```

```python
import functools

import jax
import jax.numpy as jnp
from jax import lax
from jax.experimental import pallas as pl
from jax.experimental.pallas import tpu as pltpu
from jax.sharding import PartitionSpec as P

HEAD_TOTAL = 8
HK = 128
STEPS = 2
CONV = 4
TOK = 128
PAIR = 2
MESH = pl.DeviceIdType.MESH
highest = lax.Precision.HIGHEST

NN = (((1,), (0,)), ((), ()))
NT = (((1,), (1,)), ((), ()))
TN = (((0,), (0,)), ((), ()))


def split(a):
    high = a.astype(jnp.bfloat16)
    return high, (a - high.astype(jnp.float32)).astype(jnp.bfloat16)


def dot(a, b, dims=NN):
    return lax.dot_general(a, b, dims, preferred_element_type=jnp.float32)


def dot3(a, b, dims=NN):
    (ah, al), (bh, bl) = a, b
    return dot(ah, bh, dims) + (dot(ah, bl, dims) + dot(al, bh, dims))


def unit_rows(vectors):
    return vectors * lax.rsqrt(jnp.sum(vectors * vectors, axis=-1, keepdims=True) + 1e-06)


def local_terms(heads):
    half = TOK // 2
    row = lax.broadcasted_iota(jnp.int32, (TOK, TOK), 0)
    col = lax.broadcasted_iota(jnp.int32, (TOK, TOK), 1)
    row_tok, col_tok = row & (half - 1), col & (half - 1)
    same = row_tok == col_tok
    before = (col_tok < row_tok) | (same & (col < row))
    eye = (row == col).astype(jnp.float32)

    def halves(first, second):
        return [
            jnp.concatenate([first[at : at + half], second[at : at + half]], axis=0)
            for at in (0, half)
        ]

    keys, sizes, cols, rows, grids = [], [], [], [], []
    for q, k0, k1, v0, v1, b0, b1, c_col, c_row in heads:
        keys.append([split(part) for part in halves(k0, k1)])
        sizes.append(halves(b0, b1))
        cols.append(halves(c_col, c_col))
        rows.append(
            [jnp.concatenate([c_row[:, at : at + half]] * 2, axis=1) for at in (0, half)]
        )
        (early, late) = keys[-1]
        grids.append((dot3(early, early, NT), dot3(late, late, NT), dot3(late, early, NT)))

    def faded(n, i, j, grid):
        return sizes[n][i] * jnp.exp(jnp.minimum(cols[n][i] - rows[n][j], 0.0)) * grid

    lower, below = [], []
    for n, (first, second, cross) in enumerate(grids):
        lower.append(jnp.where(before, faded(n, 0, 0, first), 0.0))
        lower.append(jnp.where(before, faded(n, 1, 1, second), 0.0))
        below.append(split(faded(n, 1, 0, cross)))
    inverse = [eye - jnp.where(same, m, 0.0) for m in lower]
    shift = 0
    while (1 << shift) < half:
        joined = ((row_tok >> (shift + 1)) == (col_tok >> (shift + 1))) & (
            (row_tok >> shift) != (col_tok >> shift)
        )
        rounded = [x.astype(jnp.bfloat16) for x in inverse]
        crosses = [jnp.where(joined, m, 0.0).astype(jnp.bfloat16) for m in lower]
        products = [dot(c, x).astype(jnp.bfloat16) for c, x in zip(crosses, rounded)]
        inverse = [x - dot(p, y) for x, p, y in zip(inverse, rounded, products)]
        shift += 1
    near = [x.astype(jnp.bfloat16) for x in inverse]
    lower = [split(m) for m in lower]

    def solve(ms, xs, sides):
        got = [dot(x, side.astype(jnp.bfloat16)) for x, side in zip(xs, sides)]
        miss = [(side - s) - dot3(m, split(s)) for side, s, m in zip(sides, got, ms)]
        return [split(s + dot(x, e.astype(jnp.bfloat16))) for s, x, e in zip(got, xs, miss)]

    sides = []
    for n, (q, k0, k1, v0, v1, b0, b1, c_col, c_row) in enumerate(heads):
        grown = jnp.exp(c_col)
        values, scaled = halves(b0 * v0, b1 * v1), halves((b0 * grown) * k0, (b1 * grown) * k1)
        sides.append([jnp.concatenate([v, k], axis=1) for v, k in zip(values, scaled)])
    tops = solve(lower[::2], near[::2], [side[0] for side in sides])
    bottoms = solve(
        lower[1::2],
        near[1::2],
        [side[1] - dot3(m, top) for side, m, top in zip(sides, below, tops)],
    )
    score_col = lax.broadcasted_iota(jnp.int32, (TOK, STEPS * TOK), 1)
    score_tok = (score_col // TOK) * half + (score_col & (half - 1))
    allowed = score_tok <= lax.broadcasted_iota(jnp.int32, (TOK, STEPS * TOK), 0)
    results = []
    for n, (q, k0, k1, v0, v1, b0, b1, c_col, c_row) in enumerate(heads):
        solved = [jnp.concatenate(pair, axis=0) for pair in zip(tops[n], bottoms[n])]
        last = c_col[TOK - 1 :, :]
        rest = jnp.exp(last - c_col)
        ends = split(jnp.concatenate(halves(k0 * rest, k1 * rest), axis=0))
        moved = dot3(solved, ends, TN)
        both = [jnp.concatenate(pair, axis=0) for pair in zip(*keys[n])]
        fade = jnp.exp(jnp.minimum(c_col - jnp.concatenate(rows[n], axis=1), 0.0))
        scores = split(jnp.where(allowed, dot3(split(q), both, NT) * fade, 0.0))
        seen = dot3(scores, solved)
        written, taken = moved[:HK], moved[HK:]
        direct, reach = seen[:, :HK], q * jnp.exp(c_col) - seen[:, HK:]
        results.append((taken, written, direct, reach, jnp.exp(last)))
    return results


def whole_kernel(
    count, sections,
    rows_ref, taps_ref, beta_ref, gate_ref, gain_ref, w_ref, out_ref,
    ext, rim, taken_hi, taken_lo, reach_hi, reach_lo, written, direct, keep,
    entering, leaving, ready, arrived, gathered,
    rim_sems, w_sems, send_sem, recv_sem, ready_send, ready_recv,
    back_send, back_recv, fore_send, fore_recv,
):
    mine, section = lax.axis_index("ctx"), lax.axis_index("section")
    after, prior = lax.rem(mine + 1, count), lax.rem(mine + count - 1, count)
    onward, behind = lax.rem(section + 1, sections), lax.rem(section + sections - 1, sections)
    fore_steps = (count - 1) // 3
    back_steps = count - 1 - fore_steps
    half_rows = w_ref.shape[0] // 2

    def remote(source, target, sends, receives, **where):
        return pltpu.make_async_remote_copy(
            src_ref=source, dst_ref=target, send_sem=sends, recv_sem=receives,
            device_id=where, device_id_type=MESH,
        )

    barrier = pltpu.get_barrier_semaphore()
    for where in ({"ctx": after}, {"ctx": prior}, {"section": onward}, {"section": behind}):
        pl.semaphore_signal(barrier, inc=1, device_id=where, device_id_type=MESH)
    pl.semaphore_wait(barrier, 4)

    edge = remote(rows_ref.at[TOK - 16 :], rim, rim_sems.at[0], rim_sems.at[1], ctx=after)
    own = remote(w_ref, gathered.at[mine], w_sems.at[0], w_sems.at[1], section=onward)

    @pl.when(mine < count - 1)
    def _():
        edge.start()

    own.start()

    def ring(send, receive, step, half, owner, target):
        block = gathered.at[owner, pl.ds(pl.multiple_of(half * half_rows, half_rows), half_rows)]
        return remote(block, block, send.at[step, half], receive.at[step, half], ctx=target)

    def back(step, half):
        return ring(back_send, back_recv, step, half, lax.rem(mine + step, count), prior)

    def fore(step, half):
        return ring(fore_send, fore_recv, step, half, lax.rem(mine + count - step, count), after)

    def relay(at, carry):
        step, half = lax.div(at, 2), lax.rem(at, 2)
        back(step - 1, half).wait_recv()
        back(step, half).start()

        @pl.when(step < fore_steps)
        def _():
            fore(step - 1, half).wait_recv()
            fore(step, half).start()

        return carry

    tok_row = lax.broadcasted_iota(jnp.int32, (TOK, TOK), 0)
    tok_col = lax.broadcasted_iota(jnp.int32, (TOK, TOK), 1)
    ones = (tok_col <= tok_row).astype(jnp.float32)
    eye = (tok_col == tok_row).astype(jnp.float32)
    gates = gate_ref[...]

    def exact(a, b):
        return lax.dot_general(a, b, NT, precision=highest, preferred_element_type=jnp.float32)

    c_cols, c_rows = exact(ones, gates), exact(gates, ones)
    betas = exact(eye, jax.nn.sigmoid(beta_ref[...]))

    def column(values, which):
        lane = lax.broadcasted_iota(jnp.int32, values.shape, 1)
        return jnp.sum(jnp.where(lane == which, values, 0.0), axis=1, keepdims=True)

    def picked_row(values, which):
        lane = lax.broadcasted_iota(jnp.int32, values.shape, 0)
        return jnp.sum(jnp.where(lane == which, values, 0.0), axis=0, keepdims=True)

    @pl.when(mine == 0)
    def _():
        rim[...] = jnp.zeros_like(rim)
        entering[...] = jnp.zeros_like(entering)

    @pl.when(mine > 0)
    def _():
        edge.wait_recv()

    width = PAIR * HK
    groups = HEAD_TOTAL // PAIR

    def hop(h, part):
        at = pl.ds(part * (HK // 2), HK // 2)
        return remote(
            leaving.at[h, at], entering.at[h, at], send_sem.at[h, part], recv_sem.at[h, part], ctx=after
        )

    def share(h):
        return remote(ready.at[h], arrived.at[h], ready_send.at[h], ready_recv.at[h], section=onward)

    def chain(h):
        moves = (taken_hi[h], taken_lo[h])
        for part in range(2):
            at = slice(part * (HK // 2), (part + 1) * (HK // 2))

            @pl.when(mine > 0)
            def _():
                hop(h, part).wait_recv()

            @pl.when(mine < count - 1)
            def _():
                state = entering[h, at]
                step = dot3(split(state), moves)
                leaving[h, at] = (keep[h][:1] * state + written[h, at]) - step
                hop(h, part).start()

        made = direct[h] + dot3((reach_hi[h], reach_lo[h]), split(entering[h]), NT)
        scale = lax.rsqrt(jnp.mean(made * made, axis=-1, keepdims=True) + 1e-05)
        gain = gain_ref[:, pl.ds(pl.multiple_of(h * HK, HK), HK)]
        ready[h] = (made * scale * gain).astype(jnp.bfloat16)
        share(h).start()

    def chain_group(g, carry):
        for p in range(PAIR):
            chain(g * PAIR + p)
        return carry

    def group(g, carry):
        first = g * PAIR

        def act(n):
            at = pl.ds(pl.multiple_of(n * (HEAD_TOTAL * HK) + g * width, width), width)
            ext[:8, :] = rim[8:, at].astype(jnp.float32)
            ext[8:, :] = rows_ref[:, at].astype(jnp.float32)
            summed = jnp.zeros((TOK, width), jnp.float32)
            taps = taps_ref[:, at].astype(jnp.float32)
            for i in range(CONV):
                start = 8 - (CONV - 1) + i
                summed = summed + taps[i : i + 1] * ext[start : start + TOK, :]
            return summed * jax.nn.sigmoid(summed)

        queries, key_0, key_1, value_0, value_1 = [act(n) for n in range(1 + 2 * STEPS)]
        heads = []
        for p in range(PAIR):
            at = slice(p * HK, (p + 1) * HK)
            heads.append(
                (
                    unit_rows(queries[:, at]),
                    unit_rows(key_0[:, at]),
                    unit_rows(key_1[:, at]),
                    value_0[:, at],
                    value_1[:, at],
                    column(betas, first + p),
                    column(betas, HEAD_TOTAL + first + p),
                    column(c_cols, first + p),
                    picked_row(c_rows, first + p),
                )
            )
        for p, (took, wrote, seen, reach, kept) in enumerate(local_terms(heads)):
            h = first + p
            taken_hi[h], taken_lo[h] = split(took)
            reach_hi[h], reach_lo[h] = split(reach)
            written[h] = wrote
            direct[h] = seen
            keep[h] = jnp.broadcast_to(kept, (8, HK))

        @pl.when(g == 0)
        def _():
            own.wait_recv()
            for half in range(2):
                back(0, half).start()
                fore(0, half).start()

        @pl.when(g > 1)
        def _():
            for half in range(2):
                relay(2 * (g - 1) + half, 0)

        @pl.when(g >= mine)
        def _():
            chain_group(g - mine, 0)

        return carry

    lax.fori_loop(0, groups, group, 0)

    ring_end = 2 * back_steps
    begin = 2 * (groups - 1)
    lead = jnp.minimum(begin + lax.div(2 * mine, 3), ring_end)
    lax.fori_loop(begin, lead, relay, 0)
    late = jnp.maximum(groups - mine, 0)

    def chain_and_ring(g, carry):
        chain_group(g, 0)

        @pl.when(lead + g - late < ring_end)
        def _():
            relay(lead + g - late, 0)

        return carry

    lax.fori_loop(late, groups, chain_and_ring, 0)
    lax.fori_loop(jnp.minimum(lead + groups - late, ring_end), ring_end, relay, 0)
    for half in range(2):
        back(back_steps - 1, half).wait_recv()
        fore(fore_steps - 1, half).wait_recv()
    for h in range(HEAD_TOTAL):
        share(h).wait_recv()
    normed = jnp.concatenate([arrived[h] for h in range(HEAD_TOTAL)], axis=1)

    def columns(n, carry):
        block = jnp.concatenate([gathered[2 * n], gathered[2 * n + 1]], axis=1)
        wide = block.shape[1]
        out_ref[:, pl.ds(pl.multiple_of(n * wide, wide), wide)] = dot(normed, block).astype(
            jnp.bfloat16
        )
        return carry

    lax.fori_loop(0, count // 2, columns, 0)

    own.wait_send()

    @pl.when(mine < count - 1)
    def _():
        edge.wait_send()
        for h in range(HEAD_TOTAL):
            for part in range(2):
                hop(h, part).wait_send()

    for h in range(HEAD_TOTAL):
        share(h).wait_send()
    for half in range(2):
        for step in range(back_steps):
            back(step, half).wait_send()
        for step in range(fore_steps):
            fore(step, half).wait_send()


def on_device(streams, conv_weight, beta_logit, gate_log, norm_gain, w_out):
    count, sections = lax.axis_size("ctx"), lax.axis_size("section")
    fore_steps = (count - 1) // 3
    back_steps = count - 1 - fore_steps
    heads = (HEAD_TOTAL, HK, HK)
    depth, share = w_out.shape[1:]
    whole = pl.BlockSpec(memory_space=pltpu.VMEM)
    dma = pltpu.SemaphoreType.DMA
    mixed = pl.pallas_call(
        functools.partial(whole_kernel, count, sections),
        in_specs=[whole] * 6,
        out_specs=whole,
        out_shape=jax.ShapeDtypeStruct((TOK, count * share), jnp.bfloat16),
        scratch_shapes=[
            pltpu.VMEM((TOK + 8, PAIR * HK), jnp.float32),
            pltpu.VMEM((16, streams.shape[2]), jnp.bfloat16),
            pltpu.VMEM(heads, jnp.bfloat16),
            pltpu.VMEM(heads, jnp.bfloat16),
            pltpu.VMEM(heads, jnp.bfloat16),
            pltpu.VMEM(heads, jnp.bfloat16),
            pltpu.VMEM(heads, jnp.float32),
            pltpu.VMEM(heads, jnp.float32),
            pltpu.VMEM((HEAD_TOTAL, 8, HK), jnp.float32),
            pltpu.VMEM(heads, jnp.float32),
            pltpu.VMEM(heads, jnp.float32),
            pltpu.VMEM(heads, jnp.bfloat16),
            pltpu.VMEM(heads, jnp.bfloat16),
            pltpu.VMEM((count, depth, share), jnp.bfloat16),
            dma((2,)),
            dma((2,)),
            dma((HEAD_TOTAL, 2)),
            dma((HEAD_TOTAL, 2)),
            dma((HEAD_TOTAL,)),
            dma((HEAD_TOTAL,)),
            dma((back_steps, 2)),
            dma((back_steps, 2)),
            dma((fore_steps, 2)),
            dma((fore_steps, 2)),
        ],
        compiler_params=pltpu.CompilerParams(
            collective_id=0, has_side_effects=True, vmem_limit_bytes=60 * 2**20
        ),
        name="whole_mixer",
    )(streams[0], conv_weight[0], beta_logit[0].T, gate_log[0].T, norm_gain, w_out[0])
    return mixed[None]


def solution(mesh):
    placed = (
        P("section", "ctx", None),
        P("section", None, None),
        P("section", "ctx", None),
        P("section", "ctx", None),
        P("section", None),
        P("section", None, "ctx"),
    )
    return jax.shard_map(
        on_device, mesh=mesh, in_specs=placed, out_specs=P("section", "ctx", None), check_vma=False
    )
```

```python
import functools

import jax
import jax.numpy as jnp
from jax import lax
from jax.experimental import pallas as pl
from jax.experimental.pallas import tpu as pltpu
from jax.sharding import PartitionSpec as P

HEAD_TOTAL = 8
HK = 128
STEPS = 2
CONV = 4
TOK = 128
PAIR = 2
MESH = pl.DeviceIdType.MESH
highest = lax.Precision.HIGHEST

NN = (((1,), (0,)), ((), ()))
NT = (((1,), (1,)), ((), ()))
TN = (((0,), (0,)), ((), ()))


def split(a):
    high = a.astype(jnp.bfloat16)
    return high, (a - high.astype(jnp.float32)).astype(jnp.bfloat16)


def dot(a, b, dims=NN):
    return lax.dot_general(a, b, dims, preferred_element_type=jnp.float32)


def dot3(a, b, dims=NN):
    (ah, al), (bh, bl) = a, b
    return dot(ah, bh, dims) + (dot(ah, bl, dims) + dot(al, bh, dims))


def unit_rows(vectors):
    return vectors * lax.rsqrt(jnp.sum(vectors * vectors, axis=-1, keepdims=True) + 1e-06)


def local_terms(heads):
    half = TOK // 2
    row = lax.broadcasted_iota(jnp.int32, (TOK, TOK), 0)
    col = lax.broadcasted_iota(jnp.int32, (TOK, TOK), 1)
    row_tok, col_tok = row & (half - 1), col & (half - 1)
    same = row_tok == col_tok
    before = (col_tok < row_tok) | (same & (col < row))
    eye = (row == col).astype(jnp.float32)

    def halves(first, second):
        return [
            jnp.concatenate([first[at : at + half], second[at : at + half]], axis=0)
            for at in (0, half)
        ]

    keys, sizes, cols, rows, grids = [], [], [], [], []
    for q, k0, k1, v0, v1, b0, b1, c_col, c_row in heads:
        keys.append([split(part) for part in halves(k0, k1)])
        sizes.append(halves(b0, b1))
        cols.append(halves(c_col, c_col))
        rows.append(
            [jnp.concatenate([c_row[:, at : at + half]] * 2, axis=1) for at in (0, half)]
        )
        (early, late) = keys[-1]
        grids.append((dot3(early, early, NT), dot3(late, late, NT), dot3(late, early, NT)))

    def faded(n, i, j, grid):
        return sizes[n][i] * jnp.exp(jnp.minimum(cols[n][i] - rows[n][j], 0.0)) * grid

    lower, below = [], []
    for n, (first, second, cross) in enumerate(grids):
        lower.append(jnp.where(before, faded(n, 0, 0, first), 0.0))
        lower.append(jnp.where(before, faded(n, 1, 1, second), 0.0))
        below.append(split(faded(n, 1, 0, cross)))
    inverse = [eye - jnp.where(same, m, 0.0) for m in lower]
    shift = 0
    while (1 << shift) < half:
        joined = ((row_tok >> (shift + 1)) == (col_tok >> (shift + 1))) & (
            (row_tok >> shift) != (col_tok >> shift)
        )
        rounded = [x.astype(jnp.bfloat16) for x in inverse]
        crosses = [jnp.where(joined, m, 0.0).astype(jnp.bfloat16) for m in lower]
        products = [dot(c, x).astype(jnp.bfloat16) for c, x in zip(crosses, rounded)]
        inverse = [x - dot(p, y) for x, p, y in zip(inverse, rounded, products)]
        shift += 1
    near = [x.astype(jnp.bfloat16) for x in inverse]
    lower = [split(m) for m in lower]

    def solve(ms, xs, sides):
        got = [dot(x, side.astype(jnp.bfloat16)) for x, side in zip(xs, sides)]
        miss = [(side - s) - dot3(m, split(s)) for side, s, m in zip(sides, got, ms)]
        return [split(s + dot(x, e.astype(jnp.bfloat16))) for s, x, e in zip(got, xs, miss)]

    sides = []
    for n, (q, k0, k1, v0, v1, b0, b1, c_col, c_row) in enumerate(heads):
        grown = jnp.exp(c_col)
        values, scaled = halves(b0 * v0, b1 * v1), halves((b0 * grown) * k0, (b1 * grown) * k1)
        sides.append([jnp.concatenate([v, k], axis=1) for v, k in zip(values, scaled)])
    tops = solve(lower[::2], near[::2], [side[0] for side in sides])
    bottoms = solve(
        lower[1::2],
        near[1::2],
        [side[1] - dot3(m, top) for side, m, top in zip(sides, below, tops)],
    )
    score_col = lax.broadcasted_iota(jnp.int32, (TOK, STEPS * TOK), 1)
    score_tok = (score_col // TOK) * half + (score_col & (half - 1))
    allowed = score_tok <= lax.broadcasted_iota(jnp.int32, (TOK, STEPS * TOK), 0)
    results = []
    for n, (q, k0, k1, v0, v1, b0, b1, c_col, c_row) in enumerate(heads):
        solved = [jnp.concatenate(pair, axis=0) for pair in zip(tops[n], bottoms[n])]
        last = c_col[TOK - 1 :, :]
        rest = jnp.exp(last - c_col)
        ends = split(jnp.concatenate(halves(k0 * rest, k1 * rest), axis=0))
        moved = dot3(solved, ends, TN)
        both = [jnp.concatenate(pair, axis=0) for pair in zip(*keys[n])]
        fade = jnp.exp(jnp.minimum(c_col - jnp.concatenate(rows[n], axis=1), 0.0))
        scores = split(jnp.where(allowed, dot3(split(q), both, NT) * fade, 0.0))
        seen = dot3(scores, solved)
        written, taken = moved[:HK], moved[HK:]
        direct, reach = seen[:, :HK], q * jnp.exp(c_col) - seen[:, HK:]
        results.append((taken, written, direct, reach, jnp.exp(last)))
    return results


def whole_kernel(
    count, sections,
    rows_ref, taps_ref, beta_ref, gate_ref, gain_ref, w_ref, out_ref,
    ext, rim, taken_hi, taken_lo, reach_hi, reach_lo, written, direct, keep,
    entering, leaving, ready, arrived, gathered, total,
    rim_sems, w_sems, send_sem, recv_sem, ready_send, ready_recv,
    back_send, back_recv, fore_send, fore_recv,
):
    mine, section = lax.axis_index("ctx"), lax.axis_index("section")
    after, prior = lax.rem(mine + 1, count), lax.rem(mine + count - 1, count)
    onward, behind = lax.rem(section + 1, sections), lax.rem(section + sections - 1, sections)
    fore_steps = 2 * (count - 1) // 5
    back_steps = count - 1 - fore_steps
    half_rows = w_ref.shape[0] // 2

    def remote(source, target, sends, receives, **where):
        return pltpu.make_async_remote_copy(
            src_ref=source, dst_ref=target, send_sem=sends, recv_sem=receives,
            device_id=where, device_id_type=MESH,
        )

    barrier = pltpu.get_barrier_semaphore()
    for where in ({"ctx": after}, {"ctx": prior}, {"section": onward}, {"section": behind}):
        pl.semaphore_signal(barrier, inc=1, device_id=where, device_id_type=MESH)
    pl.semaphore_wait(barrier, 4)

    edge = remote(rows_ref.at[TOK - 16 :], rim, rim_sems.at[0], rim_sems.at[1], ctx=after)
    own = remote(w_ref, gathered.at[mine], w_sems.at[0], w_sems.at[1], section=onward)

    @pl.when(mine < count - 1)
    def _():
        edge.start()

    own.start()

    def ring(send, receive, step, half, owner, target):
        block = gathered.at[owner, pl.ds(pl.multiple_of(half * half_rows, half_rows), half_rows)]
        return remote(block, block, send.at[step, half], receive.at[step, half], ctx=target)

    def back(step, half):
        return ring(back_send, back_recv, step, half, lax.rem(mine + step, count), prior)

    def fore(step, half):
        return ring(fore_send, fore_recv, step, half, lax.rem(mine + count - step, count), after)

    def relay(at, carry):
        step, half = lax.div(at, 2), lax.rem(at, 2)
        back(step - 1, half).wait_recv()
        back(step, half).start()

        @pl.when(step < fore_steps)
        def _():
            fore(step - 1, half).wait_recv()
            fore(step, half).start()

        return carry

    tok_row = lax.broadcasted_iota(jnp.int32, (TOK, TOK), 0)
    tok_col = lax.broadcasted_iota(jnp.int32, (TOK, TOK), 1)
    ones = (tok_col <= tok_row).astype(jnp.float32)
    eye = (tok_col == tok_row).astype(jnp.float32)
    gates = gate_ref[...]

    def exact(a, b):
        return lax.dot_general(a, b, NT, precision=highest, preferred_element_type=jnp.float32)

    c_cols, c_rows = exact(ones, gates), exact(gates, ones)
    betas = exact(eye, jax.nn.sigmoid(beta_ref[...]))

    def column(values, which):
        lane = lax.broadcasted_iota(jnp.int32, values.shape, 1)
        return jnp.sum(jnp.where(lane == which, values, 0.0), axis=1, keepdims=True)

    def picked_row(values, which):
        lane = lax.broadcasted_iota(jnp.int32, values.shape, 0)
        return jnp.sum(jnp.where(lane == which, values, 0.0), axis=0, keepdims=True)

    @pl.when(mine == 0)
    def _():
        rim[...] = jnp.zeros_like(rim)
        entering[...] = jnp.zeros_like(entering)

    @pl.when(mine > 0)
    def _():
        edge.wait_recv()

    width = PAIR * HK
    groups = HEAD_TOTAL // PAIR

    def hop(h, part):
        at = pl.ds(part * (HK // 2), HK // 2)
        return remote(
            leaving.at[h, at], entering.at[h, at], send_sem.at[h, part], recv_sem.at[h, part], ctx=after
        )

    def share(h):
        return remote(ready.at[h], arrived.at[h], ready_send.at[h], ready_recv.at[h], section=onward)

    def chain(h):
        moves = (taken_hi[h], taken_lo[h])
        for part in range(2):
            at = slice(part * (HK // 2), (part + 1) * (HK // 2))

            @pl.when(mine > 0)
            def _():
                hop(h, part).wait_recv()

            @pl.when(mine < count - 1)
            def _():
                state = entering[h, at]
                step = dot3(split(state), moves)
                leaving[h, at] = (keep[h][:1] * state + written[h, at]) - step
                hop(h, part).start()

        made = direct[h] + dot3((reach_hi[h], reach_lo[h]), split(entering[h]), NT)
        scale = lax.rsqrt(jnp.mean(made * made, axis=-1, keepdims=True) + 1e-05)
        gain = gain_ref[:, pl.ds(pl.multiple_of(h * HK, HK), HK)]
        ready[h] = (made * scale * gain).astype(jnp.bfloat16)
        share(h).start()

    def chain_group(g, carry):
        for p in range(PAIR):
            chain(g * PAIR + p)
        return carry

    def group(g, carry):
        first = g * PAIR

        def act(n):
            at = pl.ds(pl.multiple_of(n * (HEAD_TOTAL * HK) + g * width, width), width)
            ext[:8, :] = rim[8:, at].astype(jnp.float32)
            ext[8:, :] = rows_ref[:, at].astype(jnp.float32)
            summed = jnp.zeros((TOK, width), jnp.float32)
            taps = taps_ref[:, at].astype(jnp.float32)
            for i in range(CONV):
                start = 8 - (CONV - 1) + i
                summed = summed + taps[i : i + 1] * ext[start : start + TOK, :]
            return summed * jax.nn.sigmoid(summed)

        queries, key_0, key_1, value_0, value_1 = [act(n) for n in range(1 + 2 * STEPS)]
        heads = []
        for p in range(PAIR):
            at = slice(p * HK, (p + 1) * HK)
            heads.append(
                (
                    unit_rows(queries[:, at]),
                    unit_rows(key_0[:, at]),
                    unit_rows(key_1[:, at]),
                    value_0[:, at],
                    value_1[:, at],
                    column(betas, first + p),
                    column(betas, HEAD_TOTAL + first + p),
                    column(c_cols, first + p),
                    picked_row(c_rows, first + p),
                )
            )
        for p, (took, wrote, seen, reach, kept) in enumerate(local_terms(heads)):
            h = first + p
            taken_hi[h], taken_lo[h] = split(took)
            reach_hi[h], reach_lo[h] = split(reach)
            written[h] = wrote
            direct[h] = seen
            keep[h] = jnp.broadcast_to(kept, (8, HK))

        @pl.when(g == 0)
        def _():
            own.wait_recv()
            for half in range(2):
                back(0, half).start()
                fore(0, half).start()

        @pl.when(g > 1)
        def _():
            for half in range(2):
                relay(2 * (g - 1) + half, 0)

        @pl.when(g >= mine)
        def _():
            chain_group(g - mine, 0)

        return carry

    lax.fori_loop(0, groups, group, 0)

    ring_end = 2 * back_steps
    begin = 2 * (groups - 1)
    lead = jnp.minimum(begin + lax.div(2 * mine, 3), ring_end)
    lax.fori_loop(begin, lead, relay, 0)
    late = jnp.maximum(groups - mine, 0)

    def chain_and_ring(g, carry):
        chain_group(g, 0)

        @pl.when(lead + g - late < ring_end)
        def _():
            relay(lead + g - late, 0)

        return carry

    lax.fori_loop(late, groups, chain_and_ring, 0)
    lax.fori_loop(jnp.minimum(lead + groups - late, ring_end), ring_end, relay, 0)
    for half in range(2):
        back(back_steps - 1, half).wait_recv()
        fore(fore_steps - 1, half).wait_recv()
    early = HEAD_TOTAL - PAIR

    def product(heads, finish):
        for h in heads:
            share(h).wait_recv()
        normed = jnp.concatenate([arrived[h] for h in heads], axis=1)
        rows = slice(heads[0] * HK, (heads[-1] + 1) * HK)

        def columns(n, carry):
            block = jnp.concatenate([gathered[2 * n, rows], gathered[2 * n + 1, rows]], axis=1)
            wide = block.shape[1]
            finish(pl.ds(pl.multiple_of(n * wide, wide), wide), dot(normed, block))
            return carry

        lax.fori_loop(0, count // 2, columns, 0)

    def hold(at, part):
        total[:, at] = part

    def close(at, part):
        out_ref[:, at] = (total[:, at] + part).astype(jnp.bfloat16)

    product(range(early), hold)
    product(range(early, HEAD_TOTAL), close)

    own.wait_send()

    @pl.when(mine < count - 1)
    def _():
        edge.wait_send()
        for h in range(HEAD_TOTAL):
            for part in range(2):
                hop(h, part).wait_send()

    for h in range(HEAD_TOTAL):
        share(h).wait_send()
    for half in range(2):
        for step in range(back_steps):
            back(step, half).wait_send()
        for step in range(fore_steps):
            fore(step, half).wait_send()


def on_device(streams, conv_weight, beta_logit, gate_log, norm_gain, w_out):
    count, sections = lax.axis_size("ctx"), lax.axis_size("section")
    fore_steps = 2 * (count - 1) // 5
    back_steps = count - 1 - fore_steps
    heads = (HEAD_TOTAL, HK, HK)
    depth, share = w_out.shape[1:]
    whole = pl.BlockSpec(memory_space=pltpu.VMEM)
    dma = pltpu.SemaphoreType.DMA
    mixed = pl.pallas_call(
        functools.partial(whole_kernel, count, sections),
        in_specs=[whole] * 6,
        out_specs=whole,
        out_shape=jax.ShapeDtypeStruct((TOK, count * share), jnp.bfloat16),
        scratch_shapes=[
            pltpu.VMEM((TOK + 8, PAIR * HK), jnp.float32),
            pltpu.VMEM((16, streams.shape[2]), jnp.bfloat16),
            pltpu.VMEM(heads, jnp.bfloat16),
            pltpu.VMEM(heads, jnp.bfloat16),
            pltpu.VMEM(heads, jnp.bfloat16),
            pltpu.VMEM(heads, jnp.bfloat16),
            pltpu.VMEM(heads, jnp.float32),
            pltpu.VMEM(heads, jnp.float32),
            pltpu.VMEM((HEAD_TOTAL, 8, HK), jnp.float32),
            pltpu.VMEM(heads, jnp.float32),
            pltpu.VMEM(heads, jnp.float32),
            pltpu.VMEM(heads, jnp.bfloat16),
            pltpu.VMEM(heads, jnp.bfloat16),
            pltpu.VMEM((count, depth, share), jnp.bfloat16),
            pltpu.VMEM((TOK, count * share), jnp.float32),
            dma((2,)),
            dma((2,)),
            dma((HEAD_TOTAL, 2)),
            dma((HEAD_TOTAL, 2)),
            dma((HEAD_TOTAL,)),
            dma((HEAD_TOTAL,)),
            dma((back_steps, 2)),
            dma((back_steps, 2)),
            dma((fore_steps, 2)),
            dma((fore_steps, 2)),
        ],
        compiler_params=pltpu.CompilerParams(
            collective_id=0, has_side_effects=True, vmem_limit_bytes=60 * 2**20
        ),
        name="whole_mixer",
    )(streams[0], conv_weight[0], beta_logit[0].T, gate_log[0].T, norm_gain, w_out[0])
    return mixed[None]


def solution(mesh):
    placed = (
        P("section", "ctx", None),
        P("section", None, None),
        P("section", "ctx", None),
        P("section", "ctx", None),
        P("section", None),
        P("section", None, "ctx"),
    )
    return jax.shard_map(
        on_device, mesh=mesh, in_specs=placed, out_specs=P("section", "ctx", None), check_vma=False
    )
```
